32 devices in a mesh: group: 4 (over y, x), dev: 8 (over z, core).
Axes of the slice: x: 2, y: 2, z: 4, core: 2. Of those that a mesh axis runs over, the one named last changes fastest.
Arguments:
- embeddings: float32 [16384, 768], P(('group', 'dev'))
- owner: int32 [16384], P(('group', 'dev')), may hold values from 0 to 7, as said below
Outputs:
- self_max: float32 [16384], P(('group', 'dev'))
- next_max: float32 [16384], P(('group', 'dev'))
- prev_max: float32 [16384], P(('group', 'dev'))
The draws below stay inside these ranges and needn't reach their ends.
Inputs may be any that keep to these rules, and one draw needn't show every extreme that they name: `owner`: no device sends more than 128 of its vectors to one cluster; in each group one cluster takes exactly 128 vectors from every device of the group.
All inputs are finite; a program needn't handle non-finite values.
Results may differ from the reference program's by a relative error of at most 0.0004.
Values may be sent and summed in bfloat16 or wider, within the bound.
No kernel may reach another device: no remote copies, remote signals or barrier semaphores. Data moves between devices by JAX's collectives and lax.ppermute only.
A program may use at most 64 MiB of HBM per device.

```python
import jax
import jax.numpy as jnp
from jax import lax

D = 768
ROWS_DEV = 512
OWNERS = 8
GROUPS = 4
CAP = 128
VEC = 16384


def owner_table(key):

    def one_group(group_key):
        fullest = jax.random.randint(jax.random.fold_in(group_key, 1), (), 0, OWNERS).astype(jnp.int32)

        def one_source(source_key):
            others = (fullest + 1 + jnp.arange((OWNERS - 1) * CAP, dtype=jnp.int32) // CAP) % OWNERS
            picked = jax.random.permutation(jax.random.fold_in(source_key, 2), others)[:ROWS_DEV - CAP]
            listed = jnp.concatenate([jnp.full((CAP,), fullest, jnp.int32), picked.astype(jnp.int32)])
            return jax.random.permutation(jax.random.fold_in(source_key, 3), listed)
        source_keys = jax.random.split(jax.random.fold_in(group_key, 4), OWNERS)
        return jax.vmap(one_source)(source_keys)
    group_keys = jax.random.split(jax.random.fold_in(key, 77), GROUPS)
    return jax.vmap(one_group)(group_keys).reshape(VEC).astype(jnp.int32)


def draw_owner(key, part):
    return owner_table(key)


def draw_embeddings(key, part):
    ids = owner_table(key).reshape(GROUPS, OWNERS * ROWS_DEV)
    base = jax.random.normal(jax.random.fold_in(key, 11), (OWNERS, D), jnp.float32)
    moved = jax.random.normal(jax.random.fold_in(key, 12), (GROUPS, OWNERS, D), jnp.float32)
    centre = base[None, :, :] + 0.8 * moved
    group_index = jnp.arange(GROUPS, dtype=jnp.int32)[:, None]
    row_centre = centre[group_index, ids]
    spread = jnp.exp(jax.random.uniform(jax.random.fold_in(key, 13), (GROUPS, OWNERS * ROWS_DEV, 1), jnp.float32, jnp.log(0.6), jnp.log(2.5)))
    flip_draw = jax.random.uniform(jax.random.fold_in(key, 16), (GROUPS, OWNERS * ROWS_DEV, 1), jnp.float32)
    facing = jnp.where(flip_draw < 1.0 / ROWS_DEV, -1.0, 1.0).astype(jnp.float32)
    noise = jax.random.normal(jax.random.fold_in(key, 14), (GROUPS, OWNERS * ROWS_DEV, D), jnp.float32)
    values = facing * row_centre + spread * noise
    return values.reshape(VEC, D).astype(jnp.float32)


def setup_inputs(seed: int = 0) -> dict:
    keys = jax.random.split(jax.random.key(seed), 3)
    return {
        "embeddings": draw_embeddings(jax.random.fold_in(keys[2], 71), 0),
        "owner": draw_owner(jax.random.fold_in(keys[2], 71), 0),
    }


def unit_rows(embeddings):
    norm = lax.optimization_barrier(jnp.sum(embeddings * embeddings, axis=-1, keepdims=True))
    return (embeddings * lax.rsqrt(norm + 1e-06)).astype(jnp.bfloat16)

def slot_ranks(owner_rows):
    onehot = (owner_rows[:, None] == jnp.arange(OWNERS, dtype=jnp.int32)[None, :]).astype(jnp.int32)
    before = jnp.cumsum(onehot, axis=0) - onehot
    return lax.optimization_barrier(jnp.sum(before * onehot, axis=1)).astype(jnp.int32)

def pack_group(unit_group, owner_group):
    ranks = jax.vmap(slot_ranks)(owner_group)
    column = (jnp.arange(OWNERS, dtype=jnp.int32)[:, None] * CAP + ranks).astype(jnp.int32)
    slots = jnp.zeros((OWNERS, OWNERS * CAP, D), jnp.bfloat16).at[owner_group, column].set(unit_group)
    live = jnp.zeros((OWNERS, OWNERS * CAP), jnp.int32).at[owner_group, column].set(1)
    return (slots, live, column)

def best_match(left, right, live_right, skip_self):
    scores = jnp.dot(left, right.T, preferred_element_type=jnp.float32)
    keep = live_right[None, :] > 0
    if skip_self:
        size = left.shape[0]
        same = lax.broadcasted_iota(jnp.int32, (size, size), 0) == lax.broadcasted_iota(jnp.int32, (size, size), 1)
        keep = keep & jnp.logical_not(same)
    return lax.optimization_barrier(jnp.max(jnp.where(keep, scores, -1.0), axis=1))

def reference(embeddings, owner):
    unit = unit_rows(embeddings).reshape(GROUPS, OWNERS, ROWS_DEV, D)
    owner_ids = owner.reshape(GROUPS, OWNERS, ROWS_DEV)

    def per_group(group):
        later = (group + 1) % GROUPS
        earlier = (group + GROUPS - 1) % GROUPS
        slots, live, column = pack_group(unit[group], owner_ids[group])
        next_slots, next_live, unused_one = pack_group(unit[later], owner_ids[later])
        prev_slots, prev_live, unused_two = pack_group(unit[earlier], owner_ids[earlier])

        def per_cluster(cluster):
            own = slots[cluster]
            return (best_match(own, own, live[cluster], True), best_match(own, next_slots[cluster], next_live[cluster], False), best_match(own, prev_slots[cluster], prev_live[cluster], False))
        self_slot, next_slot, prev_slot = lax.map(per_cluster, jnp.arange(OWNERS, dtype=jnp.int32))
        mine = owner_ids[group]
        return (self_slot[mine, column], next_slot[mine, column], prev_slot[mine, column])
    self_all, next_all, prev_all = lax.map(per_group, jnp.arange(GROUPS, dtype=jnp.int32))
    return (self_all.reshape(VEC), next_all.reshape(VEC), prev_all.reshape(VEC))
```

```python
import functools

import jax
import jax.numpy as jnp
from jax import lax
from jax.experimental import pallas as pl
from jax.experimental.pallas import tpu as pltpu
from jax.sharding import PartitionSpec as P

BF16 = jnp.bfloat16
F32 = jnp.float32
EMPTY = 2.0
LIVE_BELOW = 1.5


def iota(shape, axis):
    return lax.broadcasted_iota(jnp.int32, shape, axis)


def dot(a, b):
    return jnp.dot(a, b, preferred_element_type=F32)


def dot_t(a, b):
    return lax.dot_general(a, b, (((1,), (1,)), ((), ())), preferred_element_type=F32)


def column_step(width):
    return next(s for s in (256, 128, width) if width % s == 0)


def pack_kernel(owners, cap, me_ref, owner_ref, rows_ref, slot_ref, *rest):
    blocks, unit_ref = rest[:-1], rest[-1]
    rows, width = rows_ref.shape
    x = rows_ref[...]
    norm = jnp.sum(x * x, axis=-1, keepdims=True)
    unit_ref[...] = (x * lax.rsqrt(norm + 1e-06)).astype(BF16)

    owner = owner_ref[...]
    held = iota((owners, rows), 0) == owner
    earlier = (iota((rows, rows), 0) < iota((rows, rows), 1)).astype(BF16)
    before = dot(held.astype(BF16), earlier)
    rank = jnp.sum(jnp.where(held, before, 0.0), axis=0, keepdims=True).astype(jnp.int32)
    slot_ref[...] = owner * cap + rank

    turned = owner ^ me_ref[0]
    place = turned * cap + rank
    pick = (iota((owners * cap, rows), 0) == place).astype(BF16)
    step = column_step(width)
    for at in range(0, width, step):
        cols = dot(pick, unit_ref[:, at : at + step])
        for k in range(owners):
            block = cols[k * cap : (k + 1) * cap]
            if at == 0:
                count = jnp.sum((turned == k).astype(jnp.int32), axis=1, keepdims=True)
                mark = (iota((cap, step), 0) >= count) & (iota((cap, step), 1) == 0)
                block = jnp.where(mark, EMPTY, block)
            blocks[k][:, at : at + step] = block.astype(BF16)


def gather_blocks(blocks, all_ref):
    at = 0
    for block in blocks:
        all_ref[at : at + block.shape[0], :] = block[...]
        at += block.shape[0]


def live_column(ref):
    return ref[:, 0:1].astype(F32) < LIVE_BELOW


def store_turned(me, out_ref, flat, cap, first=0):
    for k in range(flat.shape[1] // cap):
        out_ref[pl.ds(me ^ (first + k), 1), :] = flat[:, k * cap : (k + 1) * cap]


def self_kernel(owners, cap, me_ref, *refs):
    blocks, (out_ref, own_ref) = refs[:owners], refs[owners:]
    gather_blocks(blocks, own_ref)
    size = owners * cap
    live = live_column(own_ref)
    step = column_step(size)
    best = []
    for at in range(0, size, step):
        scores = dot_t(own_ref[...], own_ref[at : at + step, :])
        same = iota((size, step), 0) == iota((size, step), 1) + at
        keep = live & jnp.logical_not(same)
        best.append(jnp.max(jnp.where(keep, scores, -1.0), axis=0, keepdims=True))
    store_turned(me_ref[0], out_ref, jnp.concatenate(best, axis=1), cap)


def next_kernel(owners, cap, first, count, seeded, me_ref, *refs):
    own, far = refs[:owners], refs[owners : owners + count]
    rest = refs[owners + count :]
    seed_ref = rest[0] if seeded else None
    best_ref, back_ref, own_ref, far_ref = rest[1:] if seeded else rest
    gather_blocks(own, own_ref)
    gather_blocks(far, far_ref)
    size = owners * cap
    far_size = count * cap
    far_live = live_column(far_ref)
    pick_first = ((iota((8, own_ref.shape[1]), 1) == 0) & (iota((8, own_ref.shape[1]), 0) == 0)).astype(BF16)
    own_live = dot_t(pick_first, own_ref[...])[0:1] < LIVE_BELOW
    step = column_step(size)
    best = []
    back = None
    for at in range(0, size, step):
        scores = dot_t(far_ref[...], own_ref[at : at + step, :])
        best.append(jnp.max(jnp.where(far_live, scores, -1.0), axis=0, keepdims=True))
        kept = jnp.where(own_live[:, at : at + step], scores, -1.0)
        for lane in range(0, step, 128):
            part = kept[:, lane : lane + 128]
            back = part if back is None else jnp.maximum(back, part)
    me = me_ref[0]
    best = jnp.concatenate(best, axis=1)
    if seeded:
        best = jnp.maximum(best, seed_ref[...])
        store_turned(me, best_ref, best, cap)
    else:
        best_ref[...] = best
    flat = jnp.max(back.T, axis=0, keepdims=True)
    back_ref[...] = flat


def lookup_kernel(owners, cap, slot_ref, table_ref, *outs):
    rows = slot_ref.shape[1]
    size = owners * cap
    pick = (iota((size, rows), 0) == slot_ref[...]).astype(BF16)
    table = table_ref[...]
    high = table.astype(BF16)
    rest = table - high.astype(F32)
    middle = rest.astype(BF16)
    low = (rest - middle.astype(F32)).astype(BF16)
    found = (dot(low, pick) + dot(middle, pick)) + dot(high, pick)
    for i, out in enumerate(outs):
        out[...] = found[i : i + 1]


VMEM = pl.BlockSpec(memory_space=pltpu.VMEM)
SMEM = pl.BlockSpec(memory_space=pltpu.SMEM)


def call(kernel, out_shape, scratch=(), flops=0, moved=0):
    def run(*args):
        return pl.pallas_call(
            kernel,
            out_shape=out_shape,
            in_specs=[SMEM if a.ndim == 1 and a.shape[0] == 1 else VMEM for a in args],
            out_specs=jax.tree.map(lambda _: VMEM, out_shape),
            scratch_shapes=list(scratch),
            cost_estimate=pl.CostEstimate(flops=flops, bytes_accessed=moved, transcendentals=0),
        )(*args)

    return run


def local(embeddings, owner):
    owners = lax.axis_size("dev")
    groups = lax.axis_size("group")
    rows, width = embeddings.shape
    cap = max(2, 2 * rows // owners)
    size = owners * cap
    me = lax.axis_index("dev").astype(jnp.int32).reshape(1)
    struct = jax.ShapeDtypeStruct

    slot, *out = call(
        functools.partial(pack_kernel, owners, cap),
        [struct((1, rows), jnp.int32)] + [struct((cap, width), BF16)] * owners,
        [pltpu.VMEM((rows, width), BF16)],
        2 * size * rows * width,
        rows * width * 4 + size * width * 2,
    )(me, owner.reshape(1, rows), embeddings)

    def arrive(k):
        return lax.ppermute(out[k], "dev", [(i, i ^ k) for i in range(owners)])

    def forward(block):
        return lax.ppermute(block, "group", [((i + 1) % groups, i) for i in range(groups)])

    own = [out[0]]
    far = [forward(out[0])]
    for k in range(1, owners):
        own.append(arrive(k))
        far.append(forward(own[k]))

    self_best = call(
        functools.partial(self_kernel, owners, cap),
        struct((owners, cap), F32),
        [pltpu.VMEM((size, width), BF16)],
        2 * size * size * width,
        size * width * 2,
    )(me, *own)

    late = max(1, owners // 4)
    early = owners - late

    def next_call(first, count, seed):
        return call(
            functools.partial(next_kernel, owners, cap, first, count, seed is not None),
            [
                struct((1, size) if seed is None else (owners, cap), F32),
                struct((1, count * cap), F32),
            ],
            [pltpu.VMEM((size, width), BF16), pltpu.VMEM((count * cap, width), BF16)],
            2 * size * count * cap * width,
            (size + count * cap) * width * 2,
        )(me, *own, *far[first : first + count], *(() if seed is None else (seed,)))

    seed, back_early = next_call(0, early, None)
    next_best, back_late = next_call(early, late, seed)
    back = jnp.concatenate([back_early, back_late], axis=1).reshape(owners, cap)
    prev = lax.ppermute(back, "group", [(i, (i + 1) % groups) for i in range(groups)])
    prev = prev[me[0] ^ jnp.arange(owners)]
    sent = jnp.stack([self_best, next_best, prev], axis=1)
    got = lax.all_to_all(sent, "dev", split_axis=0, concat_axis=0, tiled=True)
    table = jnp.pad(jnp.swapaxes(got, 0, 1).reshape(3, size), ((0, 13), (0, 0)))
    found = call(
        functools.partial(lookup_kernel, owners, cap),
        [struct((1, rows), F32)] * 3,
        (),
        6 * 16 * size * rows,
        16 * size * 4,
    )(slot, table)
    return tuple(f.reshape(rows) for f in found)


def solution(mesh):
    placed = (P(("group", "dev"), None), P(("group", "dev")))
    return jax.shard_map(
        local,
        mesh=mesh,
        in_specs=placed,
        out_specs=(P(("group", "dev")), P(("group", "dev")), P(("group", "dev"))),
        check_vma=False,
    )
```

```python
import functools

import jax
import jax.numpy as jnp
from jax import lax
from jax.experimental import pallas as pl
from jax.experimental.pallas import tpu as pltpu
from jax.sharding import PartitionSpec as P

BF16 = jnp.bfloat16
F32 = jnp.float32
EMPTY = 2.0
LIVE_BELOW = 1.5


def iota(shape, axis):
    return lax.broadcasted_iota(jnp.int32, shape, axis)


def dot(a, b):
    return jnp.dot(a, b, preferred_element_type=F32)


def dot_t(a, b):
    return lax.dot_general(a, b, (((1,), (1,)), ((), ())), preferred_element_type=F32)


def column_step(width):
    return next(s for s in (256, 128, width) if width % s == 0)


def pack_kernel(owners, cap, me_ref, owner_ref, rows_ref, rank_ref, *rest):
    blocks, unit_ref = rest[:-1], rest[-1]
    rows, width = rows_ref.shape
    x = rows_ref[...]
    norm = jnp.sum(x * x, axis=-1, keepdims=True)
    unit_ref[...] = (x * lax.rsqrt(norm + 1e-06)).astype(BF16)

    owner = owner_ref[...]
    held = iota((owners, rows), 0) == owner
    earlier = (iota((rows, rows), 0) < iota((rows, rows), 1)).astype(BF16)
    before = dot(held.astype(BF16), earlier)
    rank = jnp.sum(jnp.where(held, before, 0.0), axis=0, keepdims=True).astype(jnp.int32)
    rank_ref[...] = rank

    turned = owner ^ me_ref[0]
    place = turned * cap + rank
    pick = (iota((owners * cap, rows), 0) == place).astype(BF16)
    step = column_step(width)
    for at in range(0, width, step):
        cols = dot(pick, unit_ref[:, at : at + step])
        for k in range(owners):
            block = cols[k * cap : (k + 1) * cap]
            if at == 0:
                count = jnp.sum((turned == k).astype(jnp.int32), axis=1, keepdims=True)
                mark = (iota((cap, step), 0) >= count) & (iota((cap, step), 1) == 0)
                block = jnp.where(mark, EMPTY, block)
            blocks[k][:, at : at + step] = block.astype(BF16)


def gather_blocks(blocks, all_ref):
    at = 0
    for block in blocks:
        all_ref[at : at + block.shape[0], :] = block[...]
        at += block.shape[0]


def live_column(ref):
    return ref[:, 0:1].astype(F32) < LIVE_BELOW


def live_lanes(ref):
    shape = (8, ref.shape[1])
    pick_first = ((iota(shape, 1) == 0) & (iota(shape, 0) == 0)).astype(BF16)
    return dot_t(pick_first, ref[...])[0:1] < LIVE_BELOW


def store_turned(me, out_ref, flat, cap):
    for k in range(flat.shape[1] // cap):
        out_ref[me ^ k] = flat[:, k * cap : (k + 1) * cap]


def self_best(own_ref):
    size = own_ref.shape[0]
    live = live_column(own_ref)
    step = column_step(size)
    best = []
    for at in range(0, size, step):
        scores = dot_t(own_ref[...], own_ref[at : at + step, :])
        same = iota((size, step), 0) == iota((size, step), 1) + at
        keep = live & jnp.logical_not(same)
        best.append(jnp.max(jnp.where(keep, scores, -1.0), axis=0, keepdims=True))
    return jnp.concatenate(best, axis=1)


def pair_best(own_ref, far_ref):
    size = own_ref.shape[0]
    far_live = live_column(far_ref)
    own_live = live_lanes(own_ref)
    step = column_step(size)
    best = []
    back = None
    for at in range(0, size, step):
        scores = dot_t(far_ref[...], own_ref[at : at + step, :])
        best.append(jnp.max(jnp.where(far_live, scores, -1.0), axis=0, keepdims=True))
        kept = jnp.where(own_live[:, at : at + step], scores, -1.0)
        for lane in range(0, step, 128):
            part = kept[:, lane : lane + 128]
            back = part if back is None else jnp.maximum(back, part)
    return jnp.concatenate(best, axis=1), jnp.max(back.T, axis=0, keepdims=True)


def early_kernel(owners, cap, early, me_ref, *refs):
    own, far = refs[:owners], refs[owners : owners + early]
    self_ref, next_ref, back_ref, own_ref, far_ref = refs[owners + early :]
    gather_blocks(own, own_ref)
    gather_blocks(far, far_ref)
    store_turned(me_ref[0], self_ref, self_best(own_ref), cap)
    next_ref[...], back_ref[...] = pair_best(own_ref, far_ref)


def late_kernel(owners, cap, late, me_ref, own_ref, seed_ref, back_seed_ref, *refs):
    far = refs[:late]
    next_ref, back_ref, far_ref = refs[late:]
    gather_blocks(far, far_ref)
    best, back = pair_best(own_ref, far_ref)
    me = me_ref[0]
    store_turned(me, next_ref, jnp.maximum(best, seed_ref[...]), cap)
    store_turned(me, back_ref, jnp.concatenate([back_seed_ref[...], back], axis=1), cap)


def lookup_kernel(owners, cap, owner_ref, rank_ref, *refs):
    tables, outs = refs[: len(refs) // 2], refs[len(refs) // 2 :]
    rows = rank_ref.shape[1]
    pick = (iota((cap, rows), 0) == rank_ref[...]).astype(BF16)
    held = iota((owners, rows), 0) == owner_ref[...]
    for table_ref, out in zip(tables, outs):
        table = jnp.concatenate([table_ref[c] for c in range(owners)], axis=0)
        high = table.astype(BF16)
        rest = table - high.astype(F32)
        middle = rest.astype(BF16)
        low = (rest - middle.astype(F32)).astype(BF16)
        found = (dot(low, pick) + dot(middle, pick)) + dot(high, pick)
        out[...] = jnp.sum(jnp.where(held, found, 0.0), axis=0, keepdims=True)


VMEM = pl.BlockSpec(memory_space=pltpu.VMEM)
SMEM = pl.BlockSpec(memory_space=pltpu.SMEM)


def call(kernel, out_shape, scratch=(), flops=0, moved=0, grant=16 << 20):
    def run(*args):
        return pl.pallas_call(
            kernel,
            out_shape=out_shape,
            in_specs=[SMEM if a.shape == (1,) else VMEM for a in args],
            out_specs=jax.tree.map(lambda _: VMEM, out_shape),
            scratch_shapes=list(scratch),
            cost_estimate=pl.CostEstimate(flops=flops, bytes_accessed=moved, transcendentals=0),
            compiler_params=pltpu.CompilerParams(vmem_limit_bytes=grant),
        )(*args)

    return run


def local(embeddings, owner):
    owners = lax.axis_size("dev")
    groups = lax.axis_size("group")
    rows, width = embeddings.shape
    cap = max(2, 2 * rows // owners)
    size = owners * cap
    me = lax.axis_index("dev").astype(jnp.int32).reshape(1)
    owner = owner.reshape(1, rows)
    struct = jax.ShapeDtypeStruct

    rank, *out = call(
        functools.partial(pack_kernel, owners, cap),
        [struct((1, rows), jnp.int32)] + [struct((cap, width), BF16)] * owners,
        [pltpu.VMEM((rows, width), BF16)],
        2 * size * rows * width,
        rows * width * 4 + size * width * 2,
    )(me, owner, embeddings)

    def arrive(k):
        return lax.ppermute(out[k], "dev", [(i, i ^ k) for i in range(owners)])

    def forward(block):
        return lax.ppermute(block, "group", [((i + 1) % groups, i) for i in range(groups)])

    half = owners // 2
    own = {k: arrive(k) for k in range(half, owners)}
    own[0] = out[0]
    far = {0: forward(own[0])}
    for k in range(1, half):
        own[k] = arrive(k)
    for k in range(1, owners):
        far[k] = forward(own[k])
    own = [own[k] for k in range(owners)]
    far = [far[k] for k in range(owners)]

    late = max(1, owners // 4)
    early = owners - late
    by_owner = struct((owners, 1, cap), F32)
    best_self, seed, back_seed, own_all = call(
        functools.partial(early_kernel, owners, cap, early),
        [by_owner, struct((1, size), F32), struct((1, early * cap), F32), struct((size, width), BF16)],
        [pltpu.VMEM((early * cap, width), BF16)],
        2 * size * (size + early * cap) * width,
        (size + early * cap) * width * 2,
    )(me, *own, *far[:early])
    best_next, back = call(
        functools.partial(late_kernel, owners, cap, late),
        [by_owner, by_owner],
        [pltpu.VMEM((late * cap, width), BF16)],
        2 * size * late * cap * width,
        (size + late * cap) * width * 2,
    )(me, own_all, seed, back_seed, *far[early:])

    def give_back(best):
        return lax.all_to_all(best, "dev", split_axis=0, concat_axis=0, tiled=True)

    prev = lax.ppermute(back, "group", [(i, (i + 1) % groups) for i in range(groups)])
    both = give_back(jnp.concatenate([best_self, best_next], axis=1))
    found = call(
        functools.partial(lookup_kernel, owners, cap),
        [struct((1, rows), F32)] * 3,
        (),
        6 * 24 * cap * rows,
        24 * cap * 4,
    )(owner, rank, both[:, 0:1], both[:, 1:2], give_back(prev))
    return tuple(f.reshape(rows) for f in found)


def solution(mesh):
    placed = (P(("group", "dev"), None), P(("group", "dev")))
    return jax.shard_map(
        local,
        mesh=mesh,
        in_specs=placed,
        out_specs=(P(("group", "dev")), P(("group", "dev")), P(("group", "dev"))),
        check_vma=False,
    )
```
